32 devices in a mesh: hid: 8 (over z, core), wid: 4 (over y, x).
Axes of the slice: x: 2, y: 2, z: 4, core: 2. Of those that a mesh axis runs over, the one named last changes fastest.
Arguments:
- grad_out: bfloat16 [64, 12288], P('hid', 'wid'), may hold values from -3 to 3
- pre_act: bfloat16 [64, 49152], P(None, 'hid'), may hold values from -6 to 6
- weight: bfloat16 [49152, 12288], P('hid', 'wid'), may hold values from -0.02734375 to 0.02734375
Outputs:
- grad_pre: bfloat16 [64, 49152], P('wid', 'hid')
- grad_weight: bfloat16 [49152, 12288], P('hid', 'wid')
The draws below stay inside these ranges and needn't reach their ends.
All inputs are finite; a program needn't handle non-finite values.
Results may differ from the reference program's by a relative error of at most 0.0051.
Values may be sent and summed in bfloat16 or wider, within the bound.
No kernel may reach another device: no remote copies, remote signals or barrier semaphores. Data moves between devices by JAX's collectives and lax.ppermute only.
A program may use at most 128 MiB of HBM per device.

```python
import math
import jax
import jax.numpy as jnp

D = 12288
FF = 49152
TOKENS = 64


def with_spikes(entries, key, source, target, shards_of, factor):
    owner, partner = [(jnp.arange(entries.shape[dim]) // (entries.shape[dim] // shards_of)).reshape([-1 if axis == dim else 1 for axis in range(entries.ndim)]) for dim in (source, target)]
    chosen = jax.random.permutation(key, shards_of)[partner]
    strong = (owner == chosen) | (owner == (partner + shards_of // 2) % shards_of)
    return jnp.where(strong, factor * entries, entries)


def block_levels(stream_key, extent, pieces, low, top_value):
    def one(axis_at, parts):
        draws = jax.random.uniform(jax.random.fold_in(jax.random.fold_in(stream_key, 6), axis_at), (parts,), jnp.float32, low / len(pieces), top_value / len(pieces))
        return jnp.repeat(jnp.exp(draws), extent[axis_at] // parts).reshape((-1,) + (1,) * (len(extent) - axis_at - 1))

    level = one(*pieces[0])
    for cut in pieces[1:]:
        level = level * one(*cut)
    return level


def gaussian(own_key, extent, deviation, most, cuts=(), dtype=jnp.bfloat16):
    array = deviation * jax.random.normal(own_key, extent, jnp.float32)
    if cuts:
        array = array * block_levels(own_key, extent, cuts, -0.22, 0.18)
    return jnp.clip(array, -most, most).astype(dtype)


def heavy_noise(stream_key, extent, spread, most, cuts, heavy, kind=jnp.bfloat16):
    result = spread * jax.random.normal(stream_key, extent, jnp.float32)
    if cuts:
        result = result * block_levels(stream_key, extent, cuts, -0.22, 0.18)
    return jnp.clip(with_spikes(result, jax.random.fold_in(stream_key, 3), *heavy), -most, most).astype(kind)


def setup_inputs(seed: int = 0) -> dict:
    key_of = jax.random.split(jax.random.key(seed), 4)
    return {
        "grad_out": heavy_noise(key_of[0], (TOKENS, D), 0.5, 3.0, ((0, 8), (1, 4)), (1, 0, 8, 2.0)),
        "pre_act": gaussian(key_of[1], (TOKENS, FF), 1.0, 6.0, ((1, 8),)),
        "weight": gaussian(key_of[2], (FF, D), FF ** -0.5, 0.02734375, ((0, 8), (1, 4))),
    }


coef = math.sqrt(2.0 / math.pi)

def gelu_parts(x):
    inner = coef * (x + 0.044715 * x * x * x)
    tangent = jnp.tanh(inner)
    value = 0.5 * x * (1.0 + tangent)
    slope = 0.5 * (1.0 + tangent) + 0.5 * x * (1.0 - tangent * tangent) * coef * (1.0 + 3.0 * 0.044715 * x * x)
    return (value, slope)

def reference(grad_out, pre_act, weight):
    value, slope = gelu_parts(pre_act.astype(jnp.float32))
    hidden = value.astype(jnp.bfloat16)
    grad_hidden = jnp.dot(grad_out, weight.T, preferred_element_type=jnp.float32)
    grad_pre = (grad_hidden * slope).astype(jnp.bfloat16)
    grad_weight = jnp.dot(hidden.T, grad_out, preferred_element_type=jnp.float32).astype(jnp.bfloat16)
    return (grad_pre, grad_weight)
```

```python
import functools
import math

import jax
import jax.numpy as jnp
from jax import lax
from jax.experimental import pallas as pl
from jax.experimental.pallas import tpu as pltpu
from jax.sharding import PartitionSpec as P

coef = math.sqrt(2.0 / math.pi)
BF16 = jnp.bfloat16
F32 = jnp.float32


def gelu_parts(x):
    inner = coef * (x + 0.044715 * x * x * x)
    tangent = jnp.tanh(inner)
    value = 0.5 * x * (1.0 + tangent)
    slope = 0.5 * (1.0 + tangent) + 0.5 * x * (1.0 - tangent * tangent) * coef * (
        1.0 + 3.0 * 0.044715 * x * x
    )
    return (value, slope)


def contract_rows(left, right):
    return lax.dot_general(
        left, right, (((0,), (0,)), ((), ())), preferred_element_type=F32
    )


def contract_cols(left, right):
    return lax.dot_general(
        left, right, (((1,), (1,)), ((), ())), preferred_element_type=F32
    )


def plain(grad_out, pre_act, weight):
    value, unused = gelu_parts(pre_act.astype(F32))
    hidden = value.astype(BF16)
    gathered = lax.all_gather(grad_out, "hid", axis=0, tiled=True)
    grad_w = contract_rows(hidden, gathered)
    partial_value = contract_cols(gathered, weight)
    share = lax.psum_scatter(partial_value, "wid", scatter_dimension=0, tiled=True)
    own_rows = share.shape[0]
    offset = lax.axis_index("wid") * own_rows
    local_pre = lax.dynamic_slice_in_dim(pre_act, offset, own_rows, 0)
    unused_value, slope = gelu_parts(local_pre.astype(F32))
    grad_pre = (share * slope).astype(BF16)
    return (grad_pre, grad_w.astype(BF16))


VMEM = pltpu.VMEM


def in_vmem():
    return pl.BlockSpec(memory_space=pltpu.VMEM)


def anywhere():
    return pl.BlockSpec(memory_space=pl.ANY)


def params(mib):
    return pltpu.CompilerParams(vmem_limit_bytes=mib * 1024 * 1024)


def gelu_kernel(parts, x_ref, hidden_ref, slope_ref):
    own = lax.axis_index("wid")
    rows = x_ref.shape[0] // parts
    for b in range(parts):
        start = pl.multiple_of(lax.bitwise_xor(own, b) * rows, rows)
        x = x_ref[pl.ds(start, rows), :].astype(F32)
        value, slope = gelu_parts(x)
        hidden_ref[b * rows : (b + 1) * rows, :] = value.astype(BF16)
        if b == 0:
            slope_ref[...] = slope


def gelu_call(parts, x):
    tokens, width = x.shape
    return pl.pallas_call(
        functools.partial(gelu_kernel, parts),
        out_shape=(
            jax.ShapeDtypeStruct((tokens, width), BF16),
            jax.ShapeDtypeStruct((tokens // parts, width), F32),
        ),
        in_specs=[in_vmem()],
        out_specs=(in_vmem(), in_vmem()),
        compiler_params=params(8),
        cost_estimate=pl.CostEstimate(
            flops=tokens * width * 20, transcendentals=tokens * width, bytes_accessed=4 * tokens * width
        ),
        name="gelu",
    )(x)


def hidden_grad_kernel(n, parts, chunks, *refs):
    own_ref, swap_ref, far_ref, farswap_ref, w_ref = refs[:5]
    g_out, own_out = refs[5:7]
    sends = refs[7 : 7 + parts - 1]
    w_buf, g_buf, sems = refs[7 + parts - 1 :]
    chunk = w_ref.shape[0] // chunks
    copies = [
        pltpu.make_async_copy(
            w_ref.at[pl.ds(i * chunk, chunk)], w_buf.at[pl.ds(i * chunk, chunk)], sems.at[i]
        )
        for i in range(chunks)
    ]
    for copy in copies:
        copy.start()
    hid = lax.axis_index("hid")
    wid = lax.axis_index("wid")
    rows = own_ref.shape[0]
    per = n // parts

    def place(source):
        block = lax.bitwise_xor(source // per, wid)
        return block * per + lax.rem(source, per)

    g_buf[place(hid)] = own_ref[...]
    g_buf[place(lax.bitwise_xor(hid, 1))] = swap_ref[...]
    for j in range(n // 2 - 1):
        k = 2 * (j + 1)
        g_buf[place(lax.bitwise_xor(hid, k))] = far_ref[j * rows : (j + 1) * rows]
        g_buf[place(lax.bitwise_xor(hid, k ^ 1))] = farswap_ref[j * rows : (j + 1) * rows]
    g = g_buf[...].reshape(n * rows, own_ref.shape[1])
    g_out[...] = g
    share = n * rows // parts
    for i, copy in enumerate(copies):
        copy.wait()
        part = contract_cols(w_buf[i * chunk : (i + 1) * chunk], g).T
        columns = slice(i * chunk, (i + 1) * chunk)
        own_out[:, columns] = part[:share]
        for k in range(1, parts):
            sends[k - 1][:, columns] = part[k * share : (k + 1) * share].astype(BF16)


def hidden_grad_call(n, parts, chunks, own, swap, far, farswap, weight):
    rows, width = own.shape
    ff = weight.shape[0]
    tokens = n * rows
    share = tokens // parts
    return pl.pallas_call(
        functools.partial(hidden_grad_kernel, n, parts, chunks),
        out_shape=(
            jax.ShapeDtypeStruct((tokens, width), BF16),
            jax.ShapeDtypeStruct((share, ff), F32),
            *[jax.ShapeDtypeStruct((share, ff), BF16)] * (parts - 1),
        ),
        in_specs=[in_vmem()] * 4 + [anywhere()],
        out_specs=tuple([in_vmem()] * (parts + 1)),
        scratch_shapes=[
            VMEM((ff, width), BF16),
            VMEM((n, rows, width), BF16),
            pltpu.SemaphoreType.DMA((chunks,)),
        ],
        compiler_params=params(48),
        cost_estimate=pl.CostEstimate(
            flops=2 * tokens * width * ff, transcendentals=0, bytes_accessed=2 * width * ff
        ),
        name="hidden_grad",
    )(own, swap, far, farswap, weight)


def weight_grad_kernel(chunks, hidden_ref, g_ref, out_ref, buf, sems):
    chunk = out_ref.shape[0] // chunks
    copies = []
    for i in range(chunks):
        rows = pl.ds(i * chunk, chunk)
        buf[i * chunk : (i + 1) * chunk] = contract_rows(
            hidden_ref[:, i * chunk : (i + 1) * chunk], g_ref[...]
        ).astype(BF16)
        copy = pltpu.make_async_copy(buf.at[rows], out_ref.at[rows], sems.at[i])
        copy.start()
        copies.append(copy)
    for copy in copies:
        copy.wait()


def weight_grad_call(chunks, hidden, g):
    tokens, ff = hidden.shape
    width = g.shape[1]
    return pl.pallas_call(
        functools.partial(weight_grad_kernel, chunks),
        out_shape=jax.ShapeDtypeStruct((ff, width), BF16),
        in_specs=[in_vmem()] * 2,
        out_specs=anywhere(),
        scratch_shapes=[VMEM((ff, width), BF16), pltpu.SemaphoreType.DMA((chunks,))],
        compiler_params=params(48),
        cost_estimate=pl.CostEstimate(
            flops=2 * tokens * width * ff, transcendentals=0, bytes_accessed=2 * width * ff
        ),
        name="weight_grad",
    )(hidden, g)


def sum_kernel(own_ref, slope_ref, *refs):
    total = own_ref[...]
    for ref in refs[:-1]:
        total = total + ref[...].astype(F32)
    refs[-1][...] = (total * slope_ref[...]).astype(BF16)


def sum_call(own, slope, received):
    return pl.pallas_call(
        sum_kernel,
        out_shape=jax.ShapeDtypeStruct(own.shape, BF16),
        in_specs=[in_vmem()] * (2 + len(received)),
        out_specs=in_vmem(),
        compiler_params=params(8),
        name="total",
    )(own, slope, *received)


def ring(n, parts, chunks, grad_out, pre_act, weight):
    def swap(value, axis, size, k):
        return lax.ppermute(value, axis, [(i, i ^ k) for i in range(size)])

    own_swap = swap(grad_out, "hid", n, 1)
    far = [swap(grad_out, "hid", n, k) for k in range(2, n, 2)]
    hidden, slope = gelu_call(parts, pre_act)
    far = jnp.concatenate(far, axis=0)
    far_swap = swap(far, "hid", n, 1)
    g, own, *sends = hidden_grad_call(n, parts, chunks, grad_out, own_swap, far, far_swap, weight)
    received = [swap(s, "wid", parts, k + 1) for k, s in enumerate(sends)]
    grad_w = weight_grad_call(chunks, hidden, g)
    return (sum_call(own, slope, received), grad_w)


def power_of_two(size):
    return size & (size - 1) == 0


def solution(mesh):
    n, parts = mesh.shape["hid"], mesh.shape["wid"]

    def local(grad_out, pre_act, weight):
        ff, width = weight.shape
        chunk = 512
        small = power_of_two(n) and power_of_two(parts) and parts < n <= 8
        if small and ff % chunk == 0 and width % 256 == 0 and ff * width * 2 <= 40 * 2**20:
            return ring(n, parts, ff // chunk, grad_out, pre_act, weight)
        return plain(grad_out, pre_act, weight)

    return jax.shard_map(
        local,
        mesh=mesh,
        in_specs=(P("hid", "wid"), P(None, "hid"), P("hid", "wid")),
        out_specs=(P("wid", "hid"), P("hid", "wid")),
        check_vma=False,
    )
```

```python
import functools
import math

import jax
import jax.numpy as jnp
from jax import lax
from jax.experimental import pallas as pl
from jax.experimental.pallas import tpu as pltpu
from jax.sharding import PartitionSpec as P

coef = math.sqrt(2.0 / math.pi)
BF16 = jnp.bfloat16
F32 = jnp.float32


def gelu_parts(x):
    inner = coef * (x + 0.044715 * x * x * x)
    tangent = jnp.tanh(inner)
    value = 0.5 * x * (1.0 + tangent)
    slope = 0.5 * (1.0 + tangent) + 0.5 * x * (1.0 - tangent * tangent) * coef * (
        1.0 + 3.0 * 0.044715 * x * x
    )
    return (value, slope)


def contract_rows(left, right):
    return lax.dot_general(
        left, right, (((0,), (0,)), ((), ())), preferred_element_type=F32
    )


def contract_cols(left, right):
    return lax.dot_general(
        left, right, (((1,), (1,)), ((), ())), preferred_element_type=F32
    )


def plain(grad_out, pre_act, weight):
    value, unused = gelu_parts(pre_act.astype(F32))
    hidden = value.astype(BF16)
    gathered = lax.all_gather(grad_out, "hid", axis=0, tiled=True)
    grad_w = contract_rows(hidden, gathered)
    partial_value = contract_cols(gathered, weight)
    share = lax.psum_scatter(partial_value, "wid", scatter_dimension=0, tiled=True)
    own_rows = share.shape[0]
    offset = lax.axis_index("wid") * own_rows
    local_pre = lax.dynamic_slice_in_dim(pre_act, offset, own_rows, 0)
    unused_value, slope = gelu_parts(local_pre.astype(F32))
    grad_pre = (share * slope).astype(BF16)
    return (grad_pre, grad_w.astype(BF16))


VMEM = pltpu.VMEM
CHUNKS = 12
EARLY = 4
GROUPS = 2


def in_vmem():
    return pl.BlockSpec(memory_space=pltpu.VMEM)


def anywhere():
    return pl.BlockSpec(memory_space=pl.ANY)


def params(mib):
    return pltpu.CompilerParams(vmem_limit_bytes=mib * 1024 * 1024)


def gelu_kernel(parts, early, x_hbm, g_hbm, w_hbm, hidden_ref, slope_ref, own_ref, w_ref, x_ref, sems):
    bring_x = pltpu.make_async_copy(x_hbm, x_ref, sems.at[0])
    bring_g = pltpu.make_async_copy(g_hbm, own_ref, sems.at[1])
    bring_x.start()
    bring_g.start()
    step = w_ref.shape[0] // early
    bring_w = []
    for i in range(early):
        rows = pl.ds(i * step, step)
        bring_w.append(pltpu.make_async_copy(w_hbm.at[rows], w_ref.at[rows], sems.at[2 + i]))
    for copy in bring_w:
        copy.start()
    bring_x.wait()
    own = lax.axis_index("wid")
    rows = x_ref.shape[0] // parts
    for b in range(parts):
        start = pl.multiple_of(lax.bitwise_xor(own, b) * rows, rows)
        x = x_ref[pl.ds(start, rows), :].astype(F32)
        value, slope = gelu_parts(x)
        hidden_ref[b * rows : (b + 1) * rows, :] = value.astype(BF16)
        if b == 0:
            slope_ref[...] = slope
    bring_g.wait()
    for copy in bring_w:
        copy.wait()


def gelu_call(parts, early, x, g, weight):
    tokens, width = x.shape
    return pl.pallas_call(
        functools.partial(gelu_kernel, parts, early),
        out_shape=(
            jax.ShapeDtypeStruct((tokens, width), BF16),
            jax.ShapeDtypeStruct((tokens // parts, width), F32),
            jax.ShapeDtypeStruct(g.shape, BF16),
            jax.ShapeDtypeStruct((weight.shape[0] * early // CHUNKS, weight.shape[1]), BF16),
        ),
        in_specs=[pl.BlockSpec(memory_space=pltpu.HBM)] * 3,
        out_specs=(in_vmem(),) * 4,
        scratch_shapes=[VMEM((tokens, width), BF16), pltpu.SemaphoreType.DMA((2 + early,))],
        compiler_params=params(8),
        cost_estimate=pl.CostEstimate(
            flops=tokens * width * 20,
            transcendentals=tokens * width,
            bytes_accessed=4 * tokens * width + weight.size * 2 * early // CHUNKS,
        ),
        name="gelu",
    )(x, g, weight)


def join_kernel(*refs):
    rows = refs[0].shape[0]
    for j, ref in enumerate(refs[:-1]):
        refs[-1][j * rows : (j + 1) * rows, :] = ref[...]


def join_call(blocks):
    rows, width = blocks[0].shape
    return pl.pallas_call(
        join_kernel,
        out_shape=jax.ShapeDtypeStruct((len(blocks) * rows, width), BF16),
        in_specs=[in_vmem()] * len(blocks),
        out_specs=in_vmem(),
        compiler_params=params(2),
        name="join",
    )(*blocks)


def hidden_grad_kernel(n, parts, early, groups, *refs):
    near_ref, swap_ref, w_hbm, held_ref = refs[:4]
    g_out, own_out = refs[4:6]
    sends = refs[6 : 6 + parts - 1]
    w_ref, g_buf, sems = refs[6 + parts - 1 :]
    late = CHUNKS - early
    step = w_ref.shape[0] // late

    def bring(i):
        source = w_hbm.at[pl.ds(pl.multiple_of((early + i) * step, step), step)]
        return pltpu.make_async_copy(source, w_ref.at[pl.ds(pl.multiple_of(i * step, step), step)], sems.at[i])

    for i in range(late):
        bring(i).start()
    hid = lax.axis_index("hid")
    wid = lax.axis_index("wid")
    rows = near_ref.shape[0] // (n // 2)
    per = n // parts

    def place(k):
        source = lax.bitwise_xor(hid, k)
        block = lax.bitwise_xor(source // per, wid)
        return block * per + lax.rem(source, per)

    for j in range(n // 2):
        g_buf[place(2 * j)] = near_ref[j * rows : (j + 1) * rows]
        g_buf[place(2 * j + 1)] = swap_ref[j * rows : (j + 1) * rows]
    g_out[...] = g_buf[...].reshape(g_out.shape)
    share = n * rows // parts

    def multiply(w, at):
        part = contract_cols(w, g_out[...]).T
        own_out[:, pl.ds(at, step)] = part[:share]
        for k in range(1, parts):
            sends[k - 1][:, pl.ds(at, step)] = part[k * share : (k + 1) * share].astype(BF16)

    for j in range(early):
        multiply(held_ref[j * step : (j + 1) * step], j * step)
    each = late // groups

    def group(i, unused):
        for j in range(each):
            bring(i * each + j).wait()
        for j in range(each):
            at = pl.multiple_of((i * each + j) * step, step)
            multiply(w_ref[pl.ds(at, step)], pl.multiple_of(at + early * step, step))
        return unused

    lax.fori_loop(0, groups, group, 0)


def hidden_grad_call(n, parts, early, groups, near, swap, weight, held):
    width = near.shape[1]
    tokens = 2 * near.shape[0]
    ff = weight.shape[0]
    share = tokens // parts
    late = CHUNKS - early
    outs = pl.pallas_call(
        functools.partial(hidden_grad_kernel, n, parts, early, groups),
        out_shape=(
            jax.ShapeDtypeStruct((tokens, width), BF16),
            jax.ShapeDtypeStruct((share, ff), F32),
            *[jax.ShapeDtypeStruct((share, ff), BF16)] * (parts - 1),
        ),
        in_specs=[in_vmem()] * 2 + [anywhere(), in_vmem()],
        out_specs=tuple([in_vmem()] * (parts + 1)),
        scratch_shapes=[
            VMEM((ff * late // CHUNKS, width), BF16),
            VMEM((n, tokens // n, width), BF16),
            pltpu.SemaphoreType.DMA((late,)),
        ],
        compiler_params=params(32),
        cost_estimate=pl.CostEstimate(
            flops=2 * tokens * width * ff, transcendentals=0, bytes_accessed=2 * width * ff
        ),
        name="hidden_grad",
    )(near, swap, weight, held)
    return outs[0], outs[1], outs[2:]


def weight_grad_kernel(chunks, hidden_ref, g_ref, out_ref, buf, sems):
    chunk = out_ref.shape[0] // chunks
    copies = []
    for i in range(chunks):
        rows = pl.ds(i * chunk, chunk)
        buf[i * chunk : (i + 1) * chunk] = contract_rows(
            hidden_ref[:, i * chunk : (i + 1) * chunk], g_ref[...]
        ).astype(BF16)
        copy = pltpu.make_async_copy(buf.at[rows], out_ref.at[rows], sems.at[i])
        copy.start()
        copies.append(copy)
    for copy in copies:
        copy.wait()


def weight_grad_call(chunks, hidden, g):
    tokens, ff = hidden.shape
    width = g.shape[1]
    return pl.pallas_call(
        functools.partial(weight_grad_kernel, chunks),
        out_shape=jax.ShapeDtypeStruct((ff, width), BF16),
        in_specs=[in_vmem()] * 2,
        out_specs=anywhere(),
        scratch_shapes=[VMEM((ff, width), BF16), pltpu.SemaphoreType.DMA((chunks,))],
        compiler_params=params(48),
        cost_estimate=pl.CostEstimate(
            flops=2 * tokens * width * ff, transcendentals=0, bytes_accessed=2 * width * ff
        ),
        name="weight_grad",
    )(hidden, g)


def sum_kernel(own_ref, slope_ref, *refs):
    total = own_ref[...]
    for ref in refs[:-1]:
        total = total + ref[...].astype(F32)
    refs[-1][...] = (total * slope_ref[...]).astype(BF16)


def sum_call(own, slope, received):
    return pl.pallas_call(
        sum_kernel,
        out_shape=jax.ShapeDtypeStruct(own.shape, BF16),
        in_specs=[in_vmem()] * (2 + len(received)),
        out_specs=in_vmem(),
        compiler_params=params(8),
        name="total",
    )(own, slope, *received)


def ring(n, parts, grad_out, pre_act, weight):
    def swap(value, axis, size, k):
        return lax.ppermute(value, axis, [(i, i ^ k) for i in range(size)])

    far = [swap(grad_out, "hid", n, k) for k in range(2, n, 2)]
    hidden, slope, own_rows, held = gelu_call(parts, EARLY, pre_act, grad_out, weight)
    near = join_call([own_rows, *far])
    other = swap(near, "hid", n, 1)
    g, own, sends = hidden_grad_call(n, parts, EARLY, GROUPS, near, other, weight, held)
    received = [swap(s, "wid", parts, k + 1) for k, s in enumerate(sends)]
    grad_w = weight_grad_call(CHUNKS, hidden, g)
    return (sum_call(own, slope, received), grad_w)


def power_of_two(size):
    return size & (size - 1) == 0


def solution(mesh):
    n, parts = mesh.shape["hid"], mesh.shape["wid"]

    def local(grad_out, pre_act, weight):
        ff, width = weight.shape
        small = power_of_two(n) and power_of_two(parts) and parts < n <= 8
        if small and ff % (CHUNKS * 256) == 0 and width % 256 == 0 and ff * width * 2 <= 40 * 2**20:
            return ring(n, parts, grad_out, pre_act, weight)
        return plain(grad_out, pre_act, weight)

    return jax.shard_map(
        local,
        mesh=mesh,
        in_specs=(P("hid", "wid"), P(None, "hid"), P("hid", "wid")),
        out_specs=(P("wid", "hid"), P("hid", "wid")),
        check_vma=False,
    )
```

```python
import functools
import math

import jax
import jax.numpy as jnp
from jax import lax
from jax.experimental import pallas as pl
from jax.experimental.pallas import tpu as pltpu
from jax.sharding import PartitionSpec as P

coef = math.sqrt(2.0 / math.pi)
BF16 = jnp.bfloat16
F32 = jnp.float32


def gelu_parts(x):
    inner = coef * (x + 0.044715 * x * x * x)
    tangent = jnp.tanh(inner)
    value = 0.5 * x * (1.0 + tangent)
    slope = 0.5 * (1.0 + tangent) + 0.5 * x * (1.0 - tangent * tangent) * coef * (
        1.0 + 3.0 * 0.044715 * x * x
    )
    return (value, slope)


def contract_rows(left, right):
    return lax.dot_general(
        left, right, (((0,), (0,)), ((), ())), preferred_element_type=F32
    )


def contract_cols(left, right):
    return lax.dot_general(
        left, right, (((1,), (1,)), ((), ())), preferred_element_type=F32
    )


def plain(grad_out, pre_act, weight):
    value, unused = gelu_parts(pre_act.astype(F32))
    hidden = value.astype(BF16)
    gathered = lax.all_gather(grad_out, "hid", axis=0, tiled=True)
    grad_w = contract_rows(hidden, gathered)
    partial_value = contract_cols(gathered, weight)
    share = lax.psum_scatter(partial_value, "wid", scatter_dimension=0, tiled=True)
    own_rows = share.shape[0]
    offset = lax.axis_index("wid") * own_rows
    local_pre = lax.dynamic_slice_in_dim(pre_act, offset, own_rows, 0)
    unused_value, slope = gelu_parts(local_pre.astype(F32))
    grad_pre = (share * slope).astype(BF16)
    return (grad_pre, grad_w.astype(BF16))


VMEM = pltpu.VMEM
CHUNKS = 12
EARLY = 3
GROUPS = 3


def in_vmem():
    return pl.BlockSpec(memory_space=pltpu.VMEM)


def anywhere():
    return pl.BlockSpec(memory_space=pl.ANY)


def params(mib):
    return pltpu.CompilerParams(vmem_limit_bytes=mib * 1024 * 1024)


def gelu_kernel(parts, early, x_hbm, g_hbm, w_hbm, hidden_ref, slope_ref, own_ref, w_ref, x_ref, sems):
    bring_x = pltpu.make_async_copy(x_hbm, x_ref, sems.at[0])
    bring_g = pltpu.make_async_copy(g_hbm, own_ref, sems.at[1])
    bring_x.start()
    bring_g.start()
    step = w_ref.shape[0] // early
    bring_w = []
    for i in range(early):
        rows = pl.ds(i * step, step)
        bring_w.append(pltpu.make_async_copy(w_hbm.at[rows], w_ref.at[rows], sems.at[2 + i]))
    for copy in bring_w:
        copy.start()
    bring_x.wait()
    own = lax.axis_index("wid")
    rows = x_ref.shape[0] // parts
    for b in range(parts):
        start = pl.multiple_of(lax.bitwise_xor(own, b) * rows, rows)
        x = x_ref[pl.ds(start, rows), :].astype(F32)
        value, slope = gelu_parts(x)
        hidden_ref[b * rows : (b + 1) * rows, :] = value.astype(BF16)
        if b == 0:
            slope_ref[...] = slope
    bring_g.wait()
    for copy in bring_w:
        copy.wait()


def gelu_call(parts, early, x, g, weight):
    tokens, width = x.shape
    return pl.pallas_call(
        functools.partial(gelu_kernel, parts, early),
        out_shape=(
            jax.ShapeDtypeStruct((tokens, width), BF16),
            jax.ShapeDtypeStruct((tokens // parts, width), F32),
            jax.ShapeDtypeStruct(g.shape, BF16),
            jax.ShapeDtypeStruct((weight.shape[0] * early // CHUNKS, weight.shape[1]), BF16),
        ),
        in_specs=[pl.BlockSpec(memory_space=pltpu.HBM)] * 3,
        out_specs=(in_vmem(),) * 4,
        scratch_shapes=[VMEM((tokens, width), BF16), pltpu.SemaphoreType.DMA((2 + early,))],
        compiler_params=params(8),
        cost_estimate=pl.CostEstimate(
            flops=tokens * width * 20,
            transcendentals=tokens * width,
            bytes_accessed=4 * tokens * width + weight.size * 2 * early // CHUNKS,
        ),
        name="gelu",
    )(*[pltpu.with_memory_space_constraint(v, pltpu.HBM) for v in (x, g, weight)])


def join_kernel(*refs):
    rows = refs[0].shape[0]
    for j, ref in enumerate(refs[:-1]):
        refs[-1][j * rows : (j + 1) * rows, :] = ref[...]


def join_call(blocks):
    rows, width = blocks[0].shape
    return pl.pallas_call(
        join_kernel,
        out_shape=jax.ShapeDtypeStruct((len(blocks) * rows, width), BF16),
        in_specs=[in_vmem()] * len(blocks),
        out_specs=in_vmem(),
        compiler_params=params(2),
        name="join",
    )(*blocks)


def hidden_grad_kernel(n, parts, early, groups, *refs):
    near_ref, swap_ref, w_hbm, held_ref = refs[:4]
    g_out, own_out = refs[4:6]
    sends = refs[6 : 6 + parts - 1]
    w_ref, g_buf, sems = refs[6 + parts - 1 :]
    late = CHUNKS - early
    step = w_ref.shape[0] // late

    def bring(i):
        source = w_hbm.at[pl.ds(pl.multiple_of((early + i) * step, step), step)]
        return pltpu.make_async_copy(source, w_ref.at[pl.ds(pl.multiple_of(i * step, step), step)], sems.at[i])

    for i in range(late):
        bring(i).start()
    hid = lax.axis_index("hid")
    wid = lax.axis_index("wid")
    rows = near_ref.shape[0] // (n // 2)
    per = n // parts

    def place(k):
        source = lax.bitwise_xor(hid, k)
        block = lax.bitwise_xor(source // per, wid)
        return block * per + lax.rem(source, per)

    for j in range(n // 2):
        g_buf[place(2 * j)] = near_ref[j * rows : (j + 1) * rows]
        g_buf[place(2 * j + 1)] = swap_ref[j * rows : (j + 1) * rows]
    g_out[...] = g_buf[...].reshape(g_out.shape)
    share = n * rows // parts

    def multiply(w, at):
        part = contract_cols(w, g_out[...]).T
        own_out[:, pl.ds(at, step)] = part[:share]
        for k in range(1, parts):
            sends[k - 1][:, pl.ds(at, step)] = part[k * share : (k + 1) * share].astype(BF16)

    for j in range(early):
        multiply(held_ref[j * step : (j + 1) * step], j * step)
    each = late // groups

    def group(i, unused):
        for j in range(each):
            bring(i * each + j).wait()
        for j in range(each):
            at = pl.multiple_of((i * each + j) * step, step)
            multiply(w_ref[pl.ds(at, step)], pl.multiple_of(at + early * step, step))
        return unused

    lax.fori_loop(0, groups, group, 0)


def hidden_grad_call(n, parts, early, groups, near, swap, weight, held):
    width = near.shape[1]
    tokens = 2 * near.shape[0]
    ff = weight.shape[0]
    share = tokens // parts
    late = CHUNKS - early
    outs = pl.pallas_call(
        functools.partial(hidden_grad_kernel, n, parts, early, groups),
        out_shape=(
            jax.ShapeDtypeStruct((tokens, width), BF16),
            jax.ShapeDtypeStruct((share, ff), F32),
            *[jax.ShapeDtypeStruct((share, ff), BF16)] * (parts - 1),
        ),
        in_specs=[in_vmem()] * 2 + [anywhere(), in_vmem()],
        out_specs=tuple([in_vmem()] * (parts + 1)),
        scratch_shapes=[
            VMEM((ff * late // CHUNKS, width), BF16),
            VMEM((n, tokens // n, width), BF16),
            pltpu.SemaphoreType.DMA((late,)),
        ],
        compiler_params=params(32),
        cost_estimate=pl.CostEstimate(
            flops=2 * tokens * width * ff, transcendentals=0, bytes_accessed=2 * width * ff
        ),
        name="hidden_grad",
    )(near, swap, weight, held)
    return outs[0], outs[1], outs[2:]


def weight_grad_kernel(sizes, hidden_ref, g_ref, out_ref, buf, sems):
    copies = []
    at = 0
    for i, size in enumerate(sizes):
        rows = pl.ds(at, size)
        buf[rows] = contract_rows(hidden_ref[:, rows], g_ref[...]).astype(BF16)
        copy = pltpu.make_async_copy(buf.at[rows], out_ref.at[rows], sems.at[i])
        copy.start()
        copies.append(copy)
        at += size
    for copy in copies:
        copy.wait()


def weight_grad_call(hidden, g):
    tokens, ff = hidden.shape
    width = g.shape[1]
    step = ff // CHUNKS
    sizes = [step // 2] * (2 * CHUNKS)
    return pl.pallas_call(
        functools.partial(weight_grad_kernel, sizes),
        out_shape=jax.ShapeDtypeStruct((ff, width), BF16),
        in_specs=[in_vmem()] * 2,
        out_specs=anywhere(),
        scratch_shapes=[VMEM((ff, width), BF16), pltpu.SemaphoreType.DMA((len(sizes),))],
        compiler_params=params(48),
        cost_estimate=pl.CostEstimate(
            flops=2 * tokens * width * ff, transcendentals=0, bytes_accessed=2 * width * ff
        ),
        name="weight_grad",
    )(hidden, g)


def sum_kernel(own_ref, slope_ref, *refs):
    total = own_ref[...]
    for ref in refs[:-1]:
        total = total + ref[...].astype(F32)
    refs[-1][...] = (total * slope_ref[...]).astype(BF16)


def sum_call(own, slope, received):
    return pl.pallas_call(
        sum_kernel,
        out_shape=jax.ShapeDtypeStruct(own.shape, BF16),
        in_specs=[in_vmem()] * (2 + len(received)),
        out_specs=in_vmem(),
        compiler_params=params(8),
        name="total",
    )(own, slope, *received)


def ring(n, parts, grad_out, pre_act, weight):
    def swap(value, axis, size, k):
        return lax.ppermute(value, axis, [(i, i ^ k) for i in range(size)])

    far = [swap(grad_out, "hid", n, k) for k in range(n - 2, 0, -2)][::-1]
    hidden, slope, own_rows, held = gelu_call(parts, EARLY, pre_act, grad_out, weight)
    near = join_call([own_rows, *far])
    other = swap(near, "hid", n, 1)
    g, own, sends = hidden_grad_call(n, parts, EARLY, GROUPS, near, other, weight, held)
    received = [swap(s, "wid", parts, k + 1) for k, s in enumerate(sends)]
    grad_w = weight_grad_call(hidden, g)
    return (sum_call(own, slope, received), grad_w)


def power_of_two(size):
    return size & (size - 1) == 0


def solution(mesh):
    n, parts = mesh.shape["hid"], mesh.shape["wid"]

    def local(grad_out, pre_act, weight):
        ff, width = weight.shape
        small = power_of_two(n) and power_of_two(parts) and parts < n <= 8
        if small and ff % (CHUNKS * 256) == 0 and width % 256 == 0 and ff * width * 2 <= 40 * 2**20:
            return ring(n, parts, grad_out, pre_act, weight)
        return plain(grad_out, pre_act, weight)

    return jax.shard_map(
        local,
        mesh=mesh,
        in_specs=(P("hid", "wid"), P(None, "hid"), P("hid", "wid")),
        out_specs=(P("wid", "hid"), P("hid", "wid")),
        check_vma=False,
    )
```

```python
import functools
import math

import jax
import jax.numpy as jnp
from jax import lax
from jax.experimental import pallas as pl
from jax.experimental.pallas import tpu as pltpu
from jax.sharding import PartitionSpec as P

coef = math.sqrt(2.0 / math.pi)
BF16 = jnp.bfloat16
F32 = jnp.float32


def gelu_parts(x):
    inner = coef * (x + 0.044715 * x * x * x)
    tangent = jnp.tanh(inner)
    value = 0.5 * x * (1.0 + tangent)
    slope = 0.5 * (1.0 + tangent) + 0.5 * x * (1.0 - tangent * tangent) * coef * (
        1.0 + 3.0 * 0.044715 * x * x
    )
    return (value, slope)


def contract_rows(left, right):
    return lax.dot_general(
        left, right, (((0,), (0,)), ((), ())), preferred_element_type=F32
    )


def contract_cols(left, right):
    return lax.dot_general(
        left, right, (((1,), (1,)), ((), ())), preferred_element_type=F32
    )


def plain(grad_out, pre_act, weight):
    value, unused = gelu_parts(pre_act.astype(F32))
    hidden = value.astype(BF16)
    gathered = lax.all_gather(grad_out, "hid", axis=0, tiled=True)
    grad_w = contract_rows(hidden, gathered)
    partial_value = contract_cols(gathered, weight)
    share = lax.psum_scatter(partial_value, "wid", scatter_dimension=0, tiled=True)
    own_rows = share.shape[0]
    offset = lax.axis_index("wid") * own_rows
    local_pre = lax.dynamic_slice_in_dim(pre_act, offset, own_rows, 0)
    unused_value, slope = gelu_parts(local_pre.astype(F32))
    grad_pre = (share * slope).astype(BF16)
    return (grad_pre, grad_w.astype(BF16))


VMEM = pltpu.VMEM
UNITS = 2
SIDE = 256
ROWS = 3 * SIDE * UNITS
SPLIT = 4
MORE = 2
BLOCKS = 24


def in_vmem():
    return pl.BlockSpec(memory_space=pltpu.VMEM)


def anywhere():
    return pl.BlockSpec(memory_space=pl.ANY)


def in_hbm(value):
    return pltpu.with_memory_space_constraint(value, pltpu.HBM)


def params(mib):
    return pltpu.CompilerParams(vmem_limit_bytes=mib * 1024 * 1024)


def piece_of(w_hbm, i):
    rows = pl.ds(pl.multiple_of((i // SPLIT) * ROWS, ROWS), ROWS)
    wide = w_hbm.shape[1] // SPLIT
    return w_hbm.at[rows, pl.ds(pl.multiple_of((i % SPLIT) * wide, wide), wide)]


def gelu_kernel(parts, x_hbm, g_hbm, w_hbm, hidden_ref, slope_ref, own_ref, w_ref, x_ref, sems):
    bring_x = pltpu.make_async_copy(x_hbm, x_ref, sems.at[0])
    bring_g = pltpu.make_async_copy(g_hbm, own_ref, sems.at[1])
    bring_x.start()
    bring_g.start()
    bring_w = [
        pltpu.make_async_copy(piece_of(w_hbm, i), w_ref.at[i], sems.at[2 + i]) for i in range(SPLIT)
    ]
    for copy in bring_w:
        copy.start()
    bring_x.wait()
    own = lax.axis_index("wid")
    rows = x_ref.shape[0] // parts
    for b in range(parts):
        start = pl.multiple_of(lax.bitwise_xor(own, b) * rows, rows)
        x = x_ref[pl.ds(start, rows), :].astype(F32)
        value, slope = gelu_parts(x)
        hidden_ref[b * rows : (b + 1) * rows, :] = value.astype(BF16)
        if b == 0:
            slope_ref[...] = slope
    bring_g.wait()
    for copy in bring_w:
        copy.wait()


def gelu_call(parts, x, g, weight):
    tokens, width = x.shape
    return pl.pallas_call(
        functools.partial(gelu_kernel, parts),
        out_shape=(
            jax.ShapeDtypeStruct((tokens, width), BF16),
            jax.ShapeDtypeStruct((tokens // parts, width), F32),
            jax.ShapeDtypeStruct(g.shape, BF16),
            jax.ShapeDtypeStruct((SPLIT, ROWS, weight.shape[1] // SPLIT), BF16),
        ),
        in_specs=[pl.BlockSpec(memory_space=pltpu.HBM)] * 3,
        out_specs=(in_vmem(),) * 4,
        scratch_shapes=[VMEM((tokens, width), BF16), pltpu.SemaphoreType.DMA((2 + SPLIT,))],
        compiler_params=params(8),
        cost_estimate=pl.CostEstimate(
            flops=tokens * width * 20,
            transcendentals=tokens * width,
            bytes_accessed=4 * tokens * width + 2 * ROWS * weight.shape[1],
        ),
        name="gelu",
    )(in_hbm(x), in_hbm(g), in_hbm(weight))


def tokens_padded(tokens):
    return -(-tokens // 128) * 128


def join_kernel(*refs):
    rows = refs[0].shape[0]
    for j, ref in enumerate(refs[:-1]):
        refs[-1][j * rows : (j + 1) * rows, :] = ref[...]


def join_call(blocks):
    rows, width = blocks[0].shape
    return pl.pallas_call(
        join_kernel,
        out_shape=jax.ShapeDtypeStruct((len(blocks) * rows, width), BF16),
        in_specs=[in_vmem()] * len(blocks),
        out_specs=in_vmem(),
        compiler_params=params(2),
        name="join",
    )(*blocks)


def fetch_kernel(near_ref, w_hbm, more_ref, sems):
    copies = [
        pltpu.make_async_copy(piece_of(w_hbm, SPLIT + i), more_ref.at[i], sems.at[i]) for i in range(MORE)
    ]
    for copy in copies:
        copy.start()
    for copy in copies:
        copy.wait()


def fetch_call(near, weight):
    wide = weight.shape[1] // SPLIT
    return pl.pallas_call(
        fetch_kernel,
        out_shape=jax.ShapeDtypeStruct((MORE, ROWS, wide), BF16),
        in_specs=[in_vmem(), anywhere()],
        out_specs=in_vmem(),
        scratch_shapes=[pltpu.SemaphoreType.DMA((MORE,))],
        compiler_params=params(2),
        cost_estimate=pl.CostEstimate(flops=0, transcendentals=0, bytes_accessed=2 * MORE * ROWS * wide),
        name="fetch",
    )(near, in_hbm(weight))


def hidden_grad_kernel(n, parts, *refs):
    near_ref, swap_ref, w_hbm, held_ref, more_ref = refs[:5]
    g_out, own_out = refs[5:7]
    sends = refs[7 : 7 + parts - 1]
    w_ref, columns_ref, g_buf, sems = refs[7 + parts - 1 :]
    first = SPLIT + MORE
    late = w_ref.shape[0]

    def bring(i):
        return pltpu.make_async_copy(piece_of(w_hbm, first + i), w_ref.at[i], sems.at[i])

    for i in range(late):
        bring(i).start()
    hid = lax.axis_index("hid")
    wid = lax.axis_index("wid")
    rows = near_ref.shape[0] // (n // 2)
    per = n // parts

    def place(k):
        source = lax.bitwise_xor(hid, k)
        block = lax.bitwise_xor(source // per, wid)
        return block * per + lax.rem(source, per)

    for j in range(n // 2):
        g_buf[place(2 * j)] = near_ref[j * rows : (j + 1) * rows]
        g_buf[place(2 * j + 1)] = swap_ref[j * rows : (j + 1) * rows]
    g_out[...] = g_buf[...].reshape(g_out.shape)
    tokens, width = g_out.shape
    columns_ref[:, :tokens] = g_out[...].T
    columns_ref[:, tokens:] = jnp.zeros_like(columns_ref[:, tokens:])
    share = tokens // parts
    block = 3 * SIDE
    steps = width // SIDE
    per_piece = steps // SPLIT

    def run(*accs):
        def hold_tokens(k):
            for m in range(UNITS):
                pltpu.matmul_push_rhs(columns_ref[pl.ds(pl.multiple_of(k * SIDE, SIDE), SIDE)], 0, m)

        def multiply(ref, part, last=False):
            for j in range(per_piece):
                k = part * per_piece + j
                here = slice(j * SIDE, (j + 1) * SIDE)
                for m in range(UNITS):
                    pltpu.matmul_acc_lhs(
                        accs[2 * m + 1], ref[m * block + SIDE : (m + 1) * block, here], load_staged_rhs=0
                    )
                for m in range(UNITS):
                    pltpu.matmul_push_rhs(ref[m * block : m * block + SIDE, here], 1, m, transpose=True)
                if not (last and j == per_piece - 1):
                    hold_tokens((k + 1) % steps)
                depth = pl.ds(pl.multiple_of(k * SIDE, SIDE), SIDE)
                for m in range(UNITS):
                    pltpu.matmul_acc_lhs(accs[2 * m], g_out[:, depth], load_staged_rhs=1)

        def store(part, at):
            columns = pl.ds(at, part.shape[1])
            own_out[:, columns] = part[:share]
            for k in range(1, parts):
                sends[k - 1][:, columns] = part[k * share : (k + 1) * share].astype(BF16)

        def finish(at):
            for m in range(UNITS):
                start = pl.multiple_of(at + m * block, SIDE)
                store(pltpu.matmul_pop(accs[2 * m]), start)
                streamed = pltpu.matmul_pop(accs[2 * m + 1])[:, : tokens_padded(tokens)]
                store(streamed.T[:tokens], pl.multiple_of(start + SIDE, SIDE))

        hold_tokens(0)
        for i in range(SPLIT):
            multiply(held_ref.at[i], i)
        finish(0)
        for i in range(MORE):
            multiply(more_ref.at[i], i)

        def piece(i, unused):
            bring(i).wait()
            at = first + i
            multiply(w_ref.at[i], at % SPLIT)

            @pl.when(at % SPLIT == SPLIT - 1)
            def _():
                finish((at // SPLIT) * ROWS)

            return unused

        lax.fori_loop(0, late - 1, piece, 0)
        bring(late - 1).wait()
        multiply(w_ref.at[late - 1], SPLIT - 1, last=True)
        finish(((first + late - 1) // SPLIT) * ROWS)

    pl.run_scoped(run, *[pltpu.ACC(m)((size, SIDE), F32) for m in range(UNITS) for size in (tokens, 2 * SIDE)])


def hidden_grad_call(n, parts, near, swap, weight, held, more):
    ff, width = weight.shape
    tokens = 2 * near.shape[0]
    share = tokens // parts
    late = ff // ROWS * SPLIT - SPLIT - MORE
    outs = pl.pallas_call(
        functools.partial(hidden_grad_kernel, n, parts),
        out_shape=(
            jax.ShapeDtypeStruct((tokens, width), BF16),
            jax.ShapeDtypeStruct((share, ff), F32),
            *[jax.ShapeDtypeStruct((share, ff), BF16)] * (parts - 1),
        ),
        in_specs=[in_vmem()] * 2 + [anywhere()] + [in_vmem()] * 2,
        out_specs=(in_vmem(),) * (parts + 1),
        scratch_shapes=[
            VMEM((late, ROWS, width // SPLIT), BF16),
            VMEM((width, SIDE), BF16),
            VMEM((n, tokens // n, width), BF16),
            pltpu.SemaphoreType.DMA((late,)),
        ],
        compiler_params=params(32),
        cost_estimate=pl.CostEstimate(
            flops=2 * tokens * width * ff, transcendentals=0, bytes_accessed=2 * width * ff
        ),
        name="hidden_grad",
    )(near, swap, in_hbm(weight), held, more)
    return outs[0], outs[1], outs[2:]


def weight_grad_kernel(sizes, hidden_ref, g_ref, out_ref, buf, sems):
    copies = []
    at = 0
    for i, size in enumerate(sizes):
        rows = pl.ds(at, size)
        buf[rows] = contract_rows(hidden_ref[:, rows], g_ref[...]).astype(BF16)
        copy = pltpu.make_async_copy(buf.at[rows], out_ref.at[rows], sems.at[i])
        copy.start()
        copies.append(copy)
        at += size
    for copy in copies:
        copy.wait()


def weight_grad_call(hidden, g):
    tokens, ff = hidden.shape
    width = g.shape[1]
    sizes = [ff // BLOCKS] * BLOCKS
    return pl.pallas_call(
        functools.partial(weight_grad_kernel, sizes),
        out_shape=jax.ShapeDtypeStruct((ff, width), BF16),
        in_specs=[in_vmem()] * 2,
        out_specs=anywhere(),
        scratch_shapes=[VMEM((ff, width), BF16), pltpu.SemaphoreType.DMA((len(sizes),))],
        compiler_params=params(48),
        cost_estimate=pl.CostEstimate(
            flops=2 * tokens * width * ff, transcendentals=0, bytes_accessed=2 * width * ff
        ),
        name="weight_grad",
    )(hidden, g)


def sum_kernel(own_ref, slope_ref, *refs):
    total = own_ref[...]
    for ref in refs[:-1]:
        total = total + ref[...].astype(F32)
    refs[-1][...] = (total * slope_ref[...]).astype(BF16)


def sum_call(own, slope, received):
    return pl.pallas_call(
        sum_kernel,
        out_shape=jax.ShapeDtypeStruct(own.shape, BF16),
        in_specs=[in_vmem()] * (2 + len(received)),
        out_specs=in_vmem(),
        compiler_params=params(8),
        name="total",
    )(own, slope, *received)


def ring(n, parts, grad_out, pre_act, weight):
    def swap(value, axis, size, k):
        return lax.ppermute(value, axis, [(i, i ^ k) for i in range(size)])

    far = [swap(grad_out, "hid", n, k) for k in range(n - 2, 0, -2)][::-1]
    hidden, slope, own_rows, held = gelu_call(parts, pre_act, grad_out, weight)
    near = join_call([own_rows, *far])
    other = swap(near, "hid", n, 1)
    more = fetch_call(near, weight)
    g, own, sends = hidden_grad_call(n, parts, near, other, weight, held, more)
    received = [swap(s, "wid", parts, k + 1) for k, s in enumerate(sends)]
    grad_w = weight_grad_call(hidden, g)
    return (sum_call(own, slope, received), grad_w)


def power_of_two(size):
    return size & (size - 1) == 0


def solution(mesh):
    n, parts = mesh.shape["hid"], mesh.shape["wid"]

    def local(grad_out, pre_act, weight):
        ff, width = weight.shape
        small = power_of_two(n) and power_of_two(parts) and parts < n <= 8
        fits = ff % ROWS == 0 and ff >= 2 * ROWS and ff % (BLOCKS * 128) == 0 and width % (SPLIT * SIDE) == 0
        if small and fits and ff * width * 2 <= 40 * 2**20:
            return ring(n, parts, grad_out, pre_act, weight)
        return plain(grad_out, pre_act, weight)

    return jax.shard_map(
        local,
        mesh=mesh,
        in_specs=(P("hid", "wid"), P(None, "hid"), P("hid", "wid")),
        out_specs=(P("wid", "hid"), P("hid", "wid")),
        check_vma=False,
    )
```

```python
import functools
import math

import jax
import jax.numpy as jnp
from jax import lax
from jax.experimental import pallas as pl
from jax.experimental.pallas import tpu as pltpu
from jax.sharding import PartitionSpec as P


coef = math.sqrt(2.0 / math.pi)
BF16 = jnp.bfloat16
F32 = jnp.float32


def gelu_parts(x):
    inner = coef * (x + 0.044715 * x * x * x)
    tangent = jnp.tanh(inner)
    value = 0.5 * x * (1.0 + tangent)
    slope = 0.5 * (1.0 + tangent) + 0.5 * x * (1.0 - tangent * tangent) * coef * (
        1.0 + 3.0 * 0.044715 * x * x
    )
    return (value, slope)


def contract_rows(left, right):
    return lax.dot_general(
        left, right, (((0,), (0,)), ((), ())), preferred_element_type=F32
    )


def contract_cols(left, right):
    return lax.dot_general(
        left, right, (((1,), (1,)), ((), ())), preferred_element_type=F32
    )


def plain(grad_out, pre_act, weight):
    value, _ = gelu_parts(pre_act.astype(F32))
    hidden = value.astype(BF16)
    gathered = lax.all_gather(grad_out, "hid", axis=0, tiled=True)
    grad_w = contract_rows(hidden, gathered)
    partial_value = contract_cols(gathered, weight)
    share = lax.psum_scatter(partial_value, "wid", scatter_dimension=0, tiled=True)
    own_rows = share.shape[0]
    offset = lax.axis_index("wid") * own_rows
    local_pre = lax.dynamic_slice_in_dim(pre_act, offset, own_rows, 0)
    _, slope = gelu_parts(local_pre.astype(F32))
    grad_pre = (share * slope).astype(BF16)
    return (grad_pre, grad_w.astype(BF16))


VMEM = pltpu.VMEM
UNITS = 2
SIDE = 256
ROWS = 3 * SIDE * UNITS
SPLIT = 4
MORE = 2
BLOCKS = 24


def in_vmem():
    return pl.BlockSpec(memory_space=pltpu.VMEM)


def anywhere():
    return pl.BlockSpec(memory_space=pl.ANY)


def in_hbm(value):
    return pltpu.with_memory_space_constraint(value, pltpu.HBM)


def params(mib):
    return pltpu.CompilerParams(vmem_limit_bytes=mib * 1024 * 1024)


def piece_of(w_hbm, i):
    rows = pl.ds(pl.multiple_of((i // SPLIT) * ROWS, ROWS), ROWS)
    wide = w_hbm.shape[1] // SPLIT
    return w_hbm.at[rows, pl.ds(pl.multiple_of((i % SPLIT) * wide, wide), wide)]


def gelu_kernel(parts, x_hbm, g_hbm, w_hbm, hidden_ref, slope_ref, own_ref, w_ref, x_ref, sems):
    bring_x = pltpu.make_async_copy(x_hbm, x_ref, sems.at[0])
    bring_g = pltpu.make_async_copy(g_hbm, own_ref, sems.at[1])
    bring_x.start()
    bring_g.start()
    bring_w = [
        pltpu.make_async_copy(piece_of(w_hbm, i), w_ref.at[i], sems.at[2 + i]) for i in range(SPLIT)
    ]
    for copy in bring_w:
        copy.start()
    bring_x.wait()
    own = lax.axis_index("wid")
    rows = x_ref.shape[0] // parts
    for b in range(parts):
        start = pl.multiple_of(lax.bitwise_xor(own, b) * rows, rows)
        x = x_ref[pl.ds(start, rows), :].astype(F32)
        value, slope = gelu_parts(x)
        hidden_ref[b * rows : (b + 1) * rows, :] = value.astype(BF16)
        if b == 0:
            slope_ref[...] = slope
    bring_g.wait()
    for copy in bring_w:
        copy.wait()


def gelu_call(parts, x, g, weight):
    tokens, width = x.shape
    return pl.pallas_call(
        functools.partial(gelu_kernel, parts),
        out_shape=(
            jax.ShapeDtypeStruct((tokens, width), BF16),
            jax.ShapeDtypeStruct((tokens // parts, width), F32),
            jax.ShapeDtypeStruct(g.shape, BF16),
            jax.ShapeDtypeStruct((SPLIT, ROWS, weight.shape[1] // SPLIT), BF16),
        ),
        in_specs=[pl.BlockSpec(memory_space=pltpu.HBM)] * 3,
        out_specs=(in_vmem(),) * 4,
        scratch_shapes=[VMEM((tokens, width), BF16), pltpu.SemaphoreType.DMA((2 + SPLIT,))],
        compiler_params=params(8),
        cost_estimate=pl.CostEstimate(
            flops=tokens * width * 20,
            transcendentals=tokens * width,
            bytes_accessed=4 * tokens * width + 2 * ROWS * weight.shape[1],
        ),
        name="gelu",
    )(in_hbm(x), in_hbm(g), in_hbm(weight))


def tokens_padded(tokens):
    return -(-tokens // 128) * 128


def join_kernel(*refs):
    rows = refs[0].shape[0]
    for j, ref in enumerate(refs[:-1]):
        refs[-1][j * rows : (j + 1) * rows, :] = ref[...]


def join_call(blocks):
    rows, width = blocks[0].shape
    return pl.pallas_call(
        join_kernel,
        out_shape=jax.ShapeDtypeStruct((len(blocks) * rows, width), BF16),
        in_specs=[in_vmem()] * len(blocks),
        out_specs=in_vmem(),
        compiler_params=params(2),
        name="join",
    )(*blocks)


def fetch_kernel(near_ref, w_hbm, more_ref, sems):
    copies = [
        pltpu.make_async_copy(piece_of(w_hbm, SPLIT + i), more_ref.at[i], sems.at[i]) for i in range(MORE)
    ]
    for copy in copies:
        copy.start()
    for copy in copies:
        copy.wait()


def fetch_call(near, weight):
    wide = weight.shape[1] // SPLIT
    return pl.pallas_call(
        fetch_kernel,
        out_shape=jax.ShapeDtypeStruct((MORE, ROWS, wide), BF16),
        in_specs=[in_vmem(), anywhere()],
        out_specs=in_vmem(),
        scratch_shapes=[pltpu.SemaphoreType.DMA((MORE,))],
        compiler_params=params(2),
        cost_estimate=pl.CostEstimate(flops=0, transcendentals=0, bytes_accessed=2 * MORE * ROWS * wide),
        name="fetch",
    )(near, in_hbm(weight))


def hidden_grad_kernel(n, parts, *refs):
    near_ref, swap_ref, w_hbm, held_ref, more_ref = refs[:5]
    g_out, own_out = refs[5:7]
    sends = refs[7 : 7 + parts - 1]
    w_ref, columns_ref, sems = refs[7 + parts - 1 :]
    first = SPLIT + MORE
    late = w_ref.shape[0]

    def bring(i):
        return pltpu.make_async_copy(piece_of(w_hbm, first + i), w_ref.at[i], sems.at[i])

    for i in range(late):
        bring(i).start()
    hid = lax.axis_index("hid")
    wid = lax.axis_index("wid")
    rows = near_ref.shape[0] // (n // 2)
    per = n // parts

    def place(k):
        source = lax.bitwise_xor(hid, k)
        block = lax.bitwise_xor(source // per, wid)
        return pl.multiple_of((block * per + lax.rem(source, per)) * rows, rows)

    for j in range(n // 2):
        g_out[pl.ds(place(2 * j), rows)] = near_ref[j * rows : (j + 1) * rows]
        g_out[pl.ds(place(2 * j + 1), rows)] = swap_ref[j * rows : (j + 1) * rows]
    tokens, width = g_out.shape
    columns_ref[:, :tokens] = g_out[...].T
    columns_ref[:, tokens:] = jnp.zeros_like(columns_ref[:, tokens:])
    share = tokens // parts
    block = 3 * SIDE
    steps = width // SIDE
    per_piece = steps // SPLIT

    def run(*accs):
        def hold_tokens(k):
            for m in range(UNITS):
                pltpu.matmul_push_rhs(columns_ref[pl.ds(pl.multiple_of(k * SIDE, SIDE), SIDE)], 0, m)

        def multiply(ref, part, last=False):
            for j in range(per_piece):
                k = part * per_piece + j
                here = slice(j * SIDE, (j + 1) * SIDE)
                for m in range(UNITS):
                    pltpu.matmul_acc_lhs(
                        accs[2 * m + 1], ref[m * block + SIDE : (m + 1) * block, here], load_staged_rhs=0
                    )
                for m in range(UNITS):
                    pltpu.matmul_push_rhs(ref[m * block : m * block + SIDE, here], 1, m, transpose=True)
                if not (last and j == per_piece - 1):
                    hold_tokens((k + 1) % steps)
                depth = pl.ds(pl.multiple_of(k * SIDE, SIDE), SIDE)
                for m in range(UNITS):
                    pltpu.matmul_acc_lhs(accs[2 * m], g_out[:, depth], load_staged_rhs=1)

        def store(part, at):
            columns = pl.ds(at, part.shape[1])
            own_out[:, columns] = part[:share]
            for k in range(1, parts):
                sends[k - 1][:, columns] = part[k * share : (k + 1) * share].astype(BF16)

        def finish(at):
            for m in range(UNITS):
                start = pl.multiple_of(at + m * block, SIDE)
                store(pltpu.matmul_pop(accs[2 * m]), start)
                streamed = pltpu.matmul_pop(accs[2 * m + 1])[:, : tokens_padded(tokens)]
                store(streamed.T[:tokens], pl.multiple_of(start + SIDE, SIDE))

        hold_tokens(0)
        for i in range(SPLIT):
            multiply(held_ref.at[i], i)
        finish(0)
        for i in range(MORE):
            multiply(more_ref.at[i], i)

        def piece(i, unused):
            bring(i).wait()
            at = first + i
            multiply(w_ref.at[i], at % SPLIT)

            @pl.when(at % SPLIT == SPLIT - 1)
            def _():
                finish((at // SPLIT) * ROWS)

            return unused

        lax.fori_loop(0, late - 1, piece, 0)
        bring(late - 1).wait()
        multiply(w_ref.at[late - 1], SPLIT - 1, last=True)
        finish(((first + late - 1) // SPLIT) * ROWS)

    pl.run_scoped(run, *[pltpu.ACC(m)((size, SIDE), F32) for m in range(UNITS) for size in (tokens, 2 * SIDE)])


def hidden_grad_call(n, parts, near, swap, weight, held, more):
    ff, width = weight.shape
    tokens = 2 * near.shape[0]
    share = tokens // parts
    late = ff // ROWS * SPLIT - SPLIT - MORE
    outs = pl.pallas_call(
        functools.partial(hidden_grad_kernel, n, parts),
        out_shape=(
            jax.ShapeDtypeStruct((tokens, width), BF16),
            jax.ShapeDtypeStruct((share, ff), F32),
            *[jax.ShapeDtypeStruct((share, ff), BF16)] * (parts - 1),
        ),
        in_specs=[in_vmem()] * 2 + [anywhere()] + [in_vmem()] * 2,
        out_specs=(in_vmem(),) * (parts + 1),
        scratch_shapes=[
            VMEM((late, ROWS, width // SPLIT), BF16),
            VMEM((width, SIDE), BF16),
            pltpu.SemaphoreType.DMA((late,)),
        ],
        compiler_params=params(32),
        cost_estimate=pl.CostEstimate(
            flops=2 * tokens * width * ff, transcendentals=0, bytes_accessed=2 * width * ff
        ),
        name="hidden_grad",
    )(near, swap, in_hbm(weight), held, more)
    return outs[0], outs[1], outs[2:]


def weight_grad_kernel(sizes, hidden_ref, g_ref, out_ref, buf, sems):
    copies = []
    at = 0
    for i, size in enumerate(sizes):
        rows = pl.ds(at, size)
        buf[rows] = contract_rows(hidden_ref[:, rows], g_ref[...]).astype(BF16)
        copy = pltpu.make_async_copy(buf.at[rows], out_ref.at[rows], sems.at[i])
        copy.start()
        copies.append(copy)
        at += size
    for copy in copies:
        copy.wait()


def weight_grad_call(hidden, g):
    tokens, ff = hidden.shape
    width = g.shape[1]
    sizes = [ff // BLOCKS] * BLOCKS
    return pl.pallas_call(
        functools.partial(weight_grad_kernel, sizes),
        out_shape=jax.ShapeDtypeStruct((ff, width), BF16),
        in_specs=[in_vmem()] * 2,
        out_specs=anywhere(),
        scratch_shapes=[VMEM((ff, width), BF16), pltpu.SemaphoreType.DMA((len(sizes),))],
        compiler_params=params(48),
        cost_estimate=pl.CostEstimate(
            flops=2 * tokens * width * ff, transcendentals=0, bytes_accessed=2 * width * ff
        ),
        name="weight_grad",
    )(hidden, g)


def sum_kernel(own_ref, slope_ref, *refs):
    total = own_ref[...]
    for ref in refs[:-1]:
        total = total + ref[...].astype(F32)
    refs[-1][...] = (total * slope_ref[...]).astype(BF16)


def sum_call(own, slope, received):
    return pl.pallas_call(
        sum_kernel,
        out_shape=jax.ShapeDtypeStruct(own.shape, BF16),
        in_specs=[in_vmem()] * (2 + len(received)),
        out_specs=in_vmem(),
        compiler_params=params(8),
        name="total",
    )(own, slope, *received)


def ring(n, parts, grad_out, pre_act, weight):
    def swap(value, axis, size, k):
        return lax.ppermute(value, axis, [(i, i ^ k) for i in range(size)])

    far = []
    for k in range(2, n, 2):
        far.append(swap(grad_out, "hid", n, k))
    hidden, slope, own_rows, held = gelu_call(parts, pre_act, grad_out, weight)
    near = join_call([own_rows, *far])
    other = swap(near, "hid", n, 1)
    more = fetch_call(near, weight)
    g, own, sends = hidden_grad_call(n, parts, near, other, weight, held, more)
    received = [swap(s, "wid", parts, k + 1) for k, s in enumerate(sends)]
    grad_w = weight_grad_call(hidden, g)
    return (sum_call(own, slope, received), grad_w)


def power_of_two(size):
    return size & (size - 1) == 0


def solution(mesh):
    n, parts = mesh.shape["hid"], mesh.shape["wid"]

    def local(grad_out, pre_act, weight):
        ff, width = weight.shape
        small = power_of_two(n) and power_of_two(parts) and parts < n <= 8
        fits = ff % ROWS == 0 and ff >= 2 * ROWS and ff % (BLOCKS * 128) == 0 and width % (SPLIT * SIDE) == 0
        if small and fits and ff * width * 2 <= 40 * 2**20:
            return ring(n, parts, grad_out, pre_act, weight)
        return plain(grad_out, pre_act, weight)

    return jax.shard_map(
        local,
        mesh=mesh,
        in_specs=(P("hid", "wid"), P(None, "hid"), P("hid", "wid")),
        out_specs=(P("wid", "hid"), P("hid", "wid")),
        check_vma=False,
    )
```

```python
import functools
import math

import jax
import jax.numpy as jnp
from jax import lax
from jax.experimental import pallas as pl
from jax.experimental.pallas import tpu as pltpu
from jax.sharding import PartitionSpec as P


coef = math.sqrt(2.0 / math.pi)
BF16 = jnp.bfloat16
F32 = jnp.float32


def gelu_parts(x):
    inner = coef * (x + 0.044715 * x * x * x)
    tangent = jnp.tanh(inner)
    value = 0.5 * x * (1.0 + tangent)
    slope = 0.5 * (1.0 + tangent) + 0.5 * x * (1.0 - tangent * tangent) * coef * (
        1.0 + 3.0 * 0.044715 * x * x
    )
    return (value, slope)


def contract_rows(left, right):
    return lax.dot_general(
        left, right, (((0,), (0,)), ((), ())), preferred_element_type=F32
    )


def contract_cols(left, right):
    return lax.dot_general(
        left, right, (((1,), (1,)), ((), ())), preferred_element_type=F32
    )


def plain(grad_out, pre_act, weight):
    value, _ = gelu_parts(pre_act.astype(F32))
    hidden = value.astype(BF16)
    gathered = lax.all_gather(grad_out, "hid", axis=0, tiled=True)
    grad_w = contract_rows(hidden, gathered)
    partial_value = contract_cols(gathered, weight)
    share = lax.psum_scatter(partial_value, "wid", scatter_dimension=0, tiled=True)
    own_rows = share.shape[0]
    offset = lax.axis_index("wid") * own_rows
    local_pre = lax.dynamic_slice_in_dim(pre_act, offset, own_rows, 0)
    _, slope = gelu_parts(local_pre.astype(F32))
    grad_pre = (share * slope).astype(BF16)
    return (grad_pre, grad_w.astype(BF16))


VMEM = pltpu.VMEM
UNITS = 2
SIDE = 256
ROWS = 3 * SIDE * UNITS
SPLIT = 6
EARLY = 7
MORE = 1
BLOCKS = 24


def in_vmem():
    return pl.BlockSpec(memory_space=pltpu.VMEM)


def anywhere():
    return pl.BlockSpec(memory_space=pl.ANY)


def in_hbm(value):
    return pltpu.with_memory_space_constraint(value, pltpu.HBM)


def params(mib):
    return pltpu.CompilerParams(vmem_limit_bytes=mib * 1024 * 1024)


def piece_of(w_hbm, i):
    rows = pl.ds(pl.multiple_of((i // SPLIT) * ROWS, ROWS), ROWS)
    wide = w_hbm.shape[1] // SPLIT
    return w_hbm.at[rows, pl.ds(pl.multiple_of((i % SPLIT) * wide, wide), wide)]


def gelu_kernel(parts, x_hbm, g_hbm, w_hbm, hidden_ref, slope_ref, own_ref, w_ref, x_ref, sems):
    bring_x = pltpu.make_async_copy(x_hbm, x_ref, sems.at[0])
    bring_g = pltpu.make_async_copy(g_hbm, own_ref, sems.at[1])
    bring_x.start()
    bring_g.start()
    bring_w = [
        pltpu.make_async_copy(piece_of(w_hbm, i), w_ref.at[i], sems.at[2 + i]) for i in range(EARLY)
    ]
    for copy in bring_w:
        copy.start()
    bring_x.wait()
    own = lax.axis_index("wid")
    rows = x_ref.shape[0] // parts
    for b in range(parts):
        start = pl.multiple_of(lax.bitwise_xor(own, b) * rows, rows)
        x = x_ref[pl.ds(start, rows), :].astype(F32)
        value, slope = gelu_parts(x)
        hidden_ref[b * rows : (b + 1) * rows, :] = value.astype(BF16)
        if b == 0:
            slope_ref[...] = slope
    bring_g.wait()
    for copy in bring_w:
        copy.wait()


def gelu_call(parts, x, g, weight):
    tokens, width = x.shape
    return pl.pallas_call(
        functools.partial(gelu_kernel, parts),
        out_shape=(
            jax.ShapeDtypeStruct((tokens, width), BF16),
            jax.ShapeDtypeStruct((tokens // parts, width), F32),
            jax.ShapeDtypeStruct(g.shape, BF16),
            jax.ShapeDtypeStruct((EARLY, ROWS, weight.shape[1] // SPLIT), BF16),
        ),
        in_specs=[pl.BlockSpec(memory_space=pltpu.HBM)] * 3,
        out_specs=(in_vmem(),) * 4,
        scratch_shapes=[VMEM((tokens, width), BF16), pltpu.SemaphoreType.DMA((2 + EARLY,))],
        compiler_params=params(8),
        cost_estimate=pl.CostEstimate(
            flops=tokens * width * 20,
            transcendentals=tokens * width,
            bytes_accessed=4 * tokens * width + 2 * ROWS * weight.shape[1] * EARLY // SPLIT,
        ),
        name="gelu",
    )(in_hbm(x), in_hbm(g), in_hbm(weight))


def tokens_padded(tokens):
    return -(-tokens // 128) * 128


def join_kernel(*refs):
    rows = refs[0].shape[0]
    for j, ref in enumerate(refs[:-1]):
        refs[-1][j * rows : (j + 1) * rows, :] = ref[...]


def join_call(blocks):
    rows, width = blocks[0].shape
    return pl.pallas_call(
        join_kernel,
        out_shape=jax.ShapeDtypeStruct((len(blocks) * rows, width), BF16),
        in_specs=[in_vmem()] * len(blocks),
        out_specs=in_vmem(),
        compiler_params=params(2),
        name="join",
    )(*blocks)


def fetch_kernel(near_ref, w_hbm, more_ref, sems):
    copies = [
        pltpu.make_async_copy(piece_of(w_hbm, EARLY + i), more_ref.at[i], sems.at[i]) for i in range(MORE)
    ]
    for copy in copies:
        copy.start()
    for copy in copies:
        copy.wait()


def fetch_call(near, weight):
    wide = weight.shape[1] // SPLIT
    return pl.pallas_call(
        fetch_kernel,
        out_shape=jax.ShapeDtypeStruct((MORE, ROWS, wide), BF16),
        in_specs=[in_vmem(), anywhere()],
        out_specs=in_vmem(),
        scratch_shapes=[pltpu.SemaphoreType.DMA((MORE,))],
        compiler_params=params(2),
        cost_estimate=pl.CostEstimate(flops=0, transcendentals=0, bytes_accessed=2 * MORE * ROWS * wide),
        name="fetch",
    )(near, in_hbm(weight))


def hidden_grad_kernel(n, parts, *refs):
    near_ref, swap_ref, w_hbm, held_ref, more_ref = refs[:5]
    g_out, own_out = refs[5:7]
    sends = refs[7 : 7 + parts - 1]
    w_ref, columns_ref, sems = refs[7 + parts - 1 :]
    first = EARLY + MORE
    late = w_ref.shape[0]

    def bring(i):
        return pltpu.make_async_copy(piece_of(w_hbm, first + i), w_ref.at[i], sems.at[i])

    for i in range(late):
        bring(i).start()
    hid = lax.axis_index("hid")
    wid = lax.axis_index("wid")
    rows = near_ref.shape[0] // (n // 2)
    per = n // parts

    def place(k):
        source = lax.bitwise_xor(hid, k)
        block = lax.bitwise_xor(source // per, wid)
        return pl.multiple_of((block * per + lax.rem(source, per)) * rows, rows)

    for j in range(n // 2):
        g_out[pl.ds(place(2 * j), rows)] = near_ref[j * rows : (j + 1) * rows]
        g_out[pl.ds(place(2 * j + 1), rows)] = swap_ref[j * rows : (j + 1) * rows]
    tokens, width = g_out.shape
    columns_ref[:, :tokens] = g_out[...].T
    columns_ref[:, tokens:] = jnp.zeros_like(columns_ref[:, tokens:])
    share = tokens // parts
    block = 3 * SIDE
    steps = width // SIDE
    per_piece = steps // SPLIT

    def run(*accs):
        def hold_tokens(k):
            for m in range(UNITS):
                pltpu.matmul_push_rhs(columns_ref[pl.ds(pl.multiple_of(k * SIDE, SIDE), SIDE)], 0, m)

        def multiply(ref, part, last=False):
            for j in range(per_piece):
                k = part * per_piece + j
                here = slice(j * SIDE, (j + 1) * SIDE)
                for m in range(UNITS):
                    pltpu.matmul_acc_lhs(
                        accs[2 * m + 1], ref[m * block + SIDE : (m + 1) * block, here], load_staged_rhs=0
                    )
                for m in range(UNITS):
                    pltpu.matmul_push_rhs(ref[m * block : m * block + SIDE, here], 1, m, transpose=True)
                if not (last and j == per_piece - 1):
                    hold_tokens((k + 1) % steps)
                depth = pl.ds(pl.multiple_of(k * SIDE, SIDE), SIDE)
                for m in range(UNITS):
                    pltpu.matmul_acc_lhs(accs[2 * m], g_out[:, depth], load_staged_rhs=1)

        def store(part, at):
            columns = pl.ds(at, part.shape[1])
            own_out[:, columns] = part[:share]
            for k in range(1, parts):
                sends[k - 1][:, columns] = part[k * share : (k + 1) * share].astype(BF16)

        def finish(at):
            for m in range(UNITS):
                start = pl.multiple_of(at + m * block, SIDE)
                store(pltpu.matmul_pop(accs[2 * m]), start)
                streamed = pltpu.matmul_pop(accs[2 * m + 1])[:, : tokens_padded(tokens)]
                store(streamed.T[:tokens], pl.multiple_of(start + SIDE, SIDE))

        hold_tokens(0)

        def held_piece(i, unused):
            multiply(held_ref.at[i], i % SPLIT)

            @pl.when(i == SPLIT - 1)
            def _():
                finish(0)

            return unused

        def more_piece(i, unused):
            multiply(more_ref.at[i], (EARLY + i) % SPLIT)
            return unused

        extra = lax.shift_right_logical(hid, 16)
        lax.fori_loop(0, EARLY + extra, held_piece, 0)
        lax.fori_loop(0, MORE + extra, more_piece, 0)

        def piece(i, unused):
            bring(i).wait()
            at = first + i
            multiply(w_ref.at[i], at % SPLIT)

            @pl.when(at % SPLIT == SPLIT - 1)
            def _():
                finish((at // SPLIT) * ROWS)

            return unused

        lax.fori_loop(0, late - 1 + extra, piece, 0)
        bring(late - 1).wait()
        multiply(w_ref.at[late - 1], SPLIT - 1, last=True)
        finish(((first + late - 1) // SPLIT) * ROWS)

    pl.run_scoped(run, *[pltpu.ACC(m)((size, SIDE), F32) for m in range(UNITS) for size in (tokens, 2 * SIDE)])


def hidden_grad_call(n, parts, near, swap, weight, held, more):
    ff, width = weight.shape
    tokens = 2 * near.shape[0]
    share = tokens // parts
    late = ff // ROWS * SPLIT - EARLY - MORE
    outs = pl.pallas_call(
        functools.partial(hidden_grad_kernel, n, parts),
        out_shape=(
            jax.ShapeDtypeStruct((tokens, width), BF16),
            jax.ShapeDtypeStruct((share, ff), F32),
            *[jax.ShapeDtypeStruct((share, ff), BF16)] * (parts - 1),
        ),
        in_specs=[in_vmem()] * 2 + [anywhere()] + [in_vmem()] * 2,
        out_specs=(in_vmem(),) * (parts + 1),
        scratch_shapes=[
            VMEM((late, ROWS, width // SPLIT), BF16),
            VMEM((width, SIDE), BF16),
            pltpu.SemaphoreType.DMA((late,)),
        ],
        compiler_params=params(32),
        cost_estimate=pl.CostEstimate(
            flops=2 * tokens * width * ff, transcendentals=0, bytes_accessed=2 * width * ff
        ),
        name="hidden_grad",
    )(near, swap, in_hbm(weight), held, more)
    return outs[0], outs[1], outs[2:]


def weight_grad_kernel(sizes, hidden_ref, g_ref, out_ref, buf, sems):
    size = sizes[0]
    pair = 4

    def send(i):
        rows = pl.ds(pl.multiple_of(i * size, size), size)
        return pltpu.make_async_copy(buf.at[rows], out_ref.at[rows], sems.at[i])

    def body(i, unused):
        for j in range(pair):
            at = i * pair + j
            rows = pl.ds(pl.multiple_of(at * size, size), size)
            buf[rows] = contract_rows(hidden_ref[:, rows], g_ref[...]).astype(BF16)
            send(at).start()
        return unused

    lax.fori_loop(0, len(sizes) // pair, body, 0)
    for i in range(len(sizes)):
        send(i).wait()


def weight_grad_call(hidden, g):
    tokens, ff = hidden.shape
    width = g.shape[1]
    sizes = [ff // BLOCKS] * BLOCKS
    return pl.pallas_call(
        functools.partial(weight_grad_kernel, sizes),
        out_shape=jax.ShapeDtypeStruct((ff, width), BF16),
        in_specs=[in_vmem()] * 2,
        out_specs=anywhere(),
        scratch_shapes=[VMEM((ff, width), BF16), pltpu.SemaphoreType.DMA((len(sizes),))],
        compiler_params=params(48),
        cost_estimate=pl.CostEstimate(
            flops=2 * tokens * width * ff, transcendentals=0, bytes_accessed=2 * width * ff
        ),
        name="weight_grad",
    )(hidden, g)


def sum_kernel(own_ref, slope_ref, *refs):
    total = own_ref[...]
    for ref in refs[:-1]:
        total = total + ref[...].astype(F32)
    refs[-1][...] = (total * slope_ref[...]).astype(BF16)


def sum_call(own, slope, received):
    return pl.pallas_call(
        sum_kernel,
        out_shape=jax.ShapeDtypeStruct(own.shape, BF16),
        in_specs=[in_vmem()] * (2 + len(received)),
        out_specs=in_vmem(),
        compiler_params=params(8),
        name="total",
    )(own, slope, *received)


def ring(n, parts, grad_out, pre_act, weight):
    def swap(value, axis, size, k):
        return lax.ppermute(value, axis, [(i, i ^ k) for i in range(size)])

    far = []
    for k in range(2, n, 2):
        far.append(swap(grad_out, "hid", n, k))
    hidden, slope, own_rows, held = gelu_call(parts, pre_act, grad_out, weight)
    near = join_call([own_rows, *far])
    other = swap(near, "hid", n, 1)
    more = fetch_call(near, weight)
    g, own, sends = hidden_grad_call(n, parts, near, other, weight, held, more)
    received = [swap(s, "wid", parts, k + 1) for k, s in enumerate(sends)]
    grad_w = weight_grad_call(hidden, g)
    return (sum_call(own, slope, received), grad_w)


def power_of_two(size):
    return size & (size - 1) == 0


def solution(mesh):
    n, parts = mesh.shape["hid"], mesh.shape["wid"]

    def local(grad_out, pre_act, weight):
        ff, width = weight.shape
        small = power_of_two(n) and power_of_two(parts) and parts < n <= 8
        fits = ff % ROWS == 0 and ff >= 3 * ROWS and ff % (BLOCKS * 128) == 0 and width % (SPLIT * SIDE) == 0
        if small and fits and ff * width * 2 <= 40 * 2**20:
            return ring(n, parts, grad_out, pre_act, weight)
        return plain(grad_out, pre_act, weight)

    return jax.shard_map(
        local,
        mesh=mesh,
        in_specs=(P("hid", "wid"), P(None, "hid"), P("hid", "wid")),
        out_specs=(P("wid", "hid"), P("hid", "wid")),
        check_vma=False,
    )
```

```python
import functools
import math

import jax
import jax.numpy as jnp
from jax import lax
from jax.experimental import pallas as pl
from jax.experimental.pallas import tpu as pltpu
from jax.sharding import PartitionSpec as P


coef = math.sqrt(2.0 / math.pi)
BF16 = jnp.bfloat16
F32 = jnp.float32


def gelu_parts(x):
    inner = coef * (x + 0.044715 * x * x * x)
    tangent = jnp.tanh(inner)
    value = 0.5 * x * (1.0 + tangent)
    slope = 0.5 * (1.0 + tangent) + 0.5 * x * (1.0 - tangent * tangent) * coef * (
        1.0 + 3.0 * 0.044715 * x * x
    )
    return (value, slope)


def contract_rows(left, right):
    return lax.dot_general(
        left, right, (((0,), (0,)), ((), ())), preferred_element_type=F32
    )


def contract_cols(left, right):
    return lax.dot_general(
        left, right, (((1,), (1,)), ((), ())), preferred_element_type=F32
    )


def plain(grad_out, pre_act, weight):
    value, _ = gelu_parts(pre_act.astype(F32))
    hidden = value.astype(BF16)
    gathered = lax.all_gather(grad_out, "hid", axis=0, tiled=True)
    grad_w = contract_rows(hidden, gathered)
    partial_value = contract_cols(gathered, weight)
    share = lax.psum_scatter(partial_value, "wid", scatter_dimension=0, tiled=True)
    own_rows = share.shape[0]
    offset = lax.axis_index("wid") * own_rows
    local_pre = lax.dynamic_slice_in_dim(pre_act, offset, own_rows, 0)
    _, slope = gelu_parts(local_pre.astype(F32))
    grad_pre = (share * slope).astype(BF16)
    return (grad_pre, grad_w.astype(BF16))


VMEM = pltpu.VMEM
UNITS = 2
SIDE = 256
ROWS = 3 * SIDE * UNITS
SPLIT = 6
EARLY = 7
MORE = 1
BLOCKS = 24


def in_vmem():
    return pl.BlockSpec(memory_space=pltpu.VMEM)


def anywhere():
    return pl.BlockSpec(memory_space=pl.ANY)


def in_hbm(value):
    return pltpu.with_memory_space_constraint(value, pltpu.HBM)


def params(mib):
    return pltpu.CompilerParams(vmem_limit_bytes=mib * 1024 * 1024)


def piece_of(w_hbm, i):
    rows = pl.ds(pl.multiple_of((i // SPLIT) * ROWS, ROWS), ROWS)
    wide = w_hbm.shape[1] // SPLIT
    return w_hbm.at[rows, pl.ds(pl.multiple_of((i % SPLIT) * wide, wide), wide)]


def gelu_kernel(parts, x_hbm, g_hbm, w_hbm, hidden_ref, slope_ref, own_ref, w_ref, x_ref, sems):
    bring_x = pltpu.make_async_copy(x_hbm, x_ref, sems.at[0])
    bring_g = pltpu.make_async_copy(g_hbm, own_ref, sems.at[1])
    bring_x.start()
    bring_g.start()
    bring_w = [
        pltpu.make_async_copy(piece_of(w_hbm, i), w_ref.at[i], sems.at[2 + i]) for i in range(EARLY)
    ]
    for copy in bring_w:
        copy.start()
    bring_x.wait()
    own = lax.axis_index("wid")
    rows = x_ref.shape[0] // parts
    for b in range(parts):
        start = pl.multiple_of(lax.bitwise_xor(own, b) * rows, rows)
        x = x_ref[pl.ds(start, rows), :].astype(F32)
        value, slope = gelu_parts(x)
        hidden_ref[b * rows : (b + 1) * rows, :] = value.astype(BF16)
        if b == 0:
            slope_ref[...] = slope
    bring_g.wait()
    for copy in bring_w:
        copy.wait()


def gelu_call(parts, x, g, weight):
    tokens, width = x.shape
    return pl.pallas_call(
        functools.partial(gelu_kernel, parts),
        out_shape=(
            jax.ShapeDtypeStruct((tokens, width), BF16),
            jax.ShapeDtypeStruct((tokens // parts, width), F32),
            jax.ShapeDtypeStruct(g.shape, BF16),
            jax.ShapeDtypeStruct((EARLY, ROWS, weight.shape[1] // SPLIT), BF16),
        ),
        in_specs=[pl.BlockSpec(memory_space=pltpu.HBM)] * 3,
        out_specs=(in_vmem(),) * 4,
        scratch_shapes=[VMEM((tokens, width), BF16), pltpu.SemaphoreType.DMA((2 + EARLY,))],
        compiler_params=params(8),
        cost_estimate=pl.CostEstimate(
            flops=tokens * width * 20,
            transcendentals=tokens * width,
            bytes_accessed=4 * tokens * width + 2 * ROWS * weight.shape[1] * EARLY // SPLIT,
        ),
        name="gelu",
    )(in_hbm(x), in_hbm(g), in_hbm(weight))


def tokens_padded(tokens):
    return -(-tokens // 128) * 128


def join_kernel(*refs):
    rows = refs[0].shape[0]
    for j, ref in enumerate(refs[:-1]):
        refs[-1][j * rows : (j + 1) * rows, :] = ref[...]


def join_call(blocks):
    rows, width = blocks[0].shape
    return pl.pallas_call(
        join_kernel,
        out_shape=jax.ShapeDtypeStruct((len(blocks) * rows, width), BF16),
        in_specs=[in_vmem()] * len(blocks),
        out_specs=in_vmem(),
        compiler_params=params(2),
        name="join",
    )(*blocks)


def fetch_kernel(near_ref, w_hbm, more_ref, sems):
    copies = [
        pltpu.make_async_copy(piece_of(w_hbm, EARLY + i), more_ref.at[i], sems.at[i]) for i in range(MORE)
    ]
    for copy in copies:
        copy.start()
    for copy in copies:
        copy.wait()


def fetch_call(near, weight):
    wide = weight.shape[1] // SPLIT
    return pl.pallas_call(
        fetch_kernel,
        out_shape=jax.ShapeDtypeStruct((MORE, ROWS, wide), BF16),
        in_specs=[in_vmem(), anywhere()],
        out_specs=in_vmem(),
        scratch_shapes=[pltpu.SemaphoreType.DMA((MORE,))],
        compiler_params=params(2),
        cost_estimate=pl.CostEstimate(flops=0, transcendentals=0, bytes_accessed=2 * MORE * ROWS * wide),
        name="fetch",
    )(near, in_hbm(weight))


def hidden_grad_kernel(n, parts, *refs):
    near_ref, swap_ref, w_hbm, held_ref, more_ref = refs[:5]
    g_out, own_out = refs[5:7]
    sends = refs[7 : 7 + parts - 1]
    w_ref, columns_ref, sems = refs[7 + parts - 1 :]
    first = EARLY + MORE
    late = w_ref.shape[0]

    def bring(i):
        return pltpu.make_async_copy(piece_of(w_hbm, first + i), w_ref.at[i], sems.at[i])

    for i in range(late):
        bring(i).start()
    hid = lax.axis_index("hid")
    wid = lax.axis_index("wid")
    rows = near_ref.shape[0] // (n // 2)
    per = n // parts

    def place(k):
        source = lax.bitwise_xor(hid, k)
        block = lax.bitwise_xor(source // per, wid)
        return pl.multiple_of((block * per + lax.rem(source, per)) * rows, rows)

    for j in range(n // 2):
        g_out[pl.ds(place(2 * j), rows)] = near_ref[j * rows : (j + 1) * rows]
        g_out[pl.ds(place(2 * j + 1), rows)] = swap_ref[j * rows : (j + 1) * rows]
    tokens, width = g_out.shape
    columns_ref[:, :tokens] = g_out[...].T
    columns_ref[:, tokens:] = jnp.zeros_like(columns_ref[:, tokens:])
    share = tokens // parts
    block = 3 * SIDE
    steps = width // SIDE
    per_piece = steps // SPLIT

    def run(*accs):
        def hold_tokens(k):
            for m in range(UNITS):
                pltpu.matmul_push_rhs(columns_ref[pl.ds(pl.multiple_of(k * SIDE, SIDE), SIDE)], 0, m)

        def multiply(ref, part, last=False):
            for j in range(per_piece):
                k = part * per_piece + j
                here = slice(j * SIDE, (j + 1) * SIDE)
                for m in range(UNITS):
                    pltpu.matmul_acc_lhs(
                        accs[2 * m + 1], ref[m * block + SIDE : (m + 1) * block, here], load_staged_rhs=0
                    )
                for m in range(UNITS):
                    pltpu.matmul_push_rhs(ref[m * block : m * block + SIDE, here], 1, m, transpose=True)
                if not (last and j == per_piece - 1):
                    hold_tokens((k + 1) % steps)
                depth = pl.ds(pl.multiple_of(k * SIDE, SIDE), SIDE)
                for m in range(UNITS):
                    pltpu.matmul_acc_lhs(accs[2 * m], g_out[:, depth], load_staged_rhs=1)

        def store(part, at):
            columns = pl.ds(at, part.shape[1])
            own_out[:, columns] = part[:share]
            for k in range(1, parts):
                sends[k - 1][:, columns] = part[k * share : (k + 1) * share].astype(BF16)

        def finish(at):
            for m in range(UNITS):
                start = pl.multiple_of(at + m * block, SIDE)
                store(pltpu.matmul_pop(accs[2 * m]), start)
                streamed = pltpu.matmul_pop(accs[2 * m + 1])[:, : tokens_padded(tokens)]
                store(streamed.T[:tokens], pl.multiple_of(start + SIDE, SIDE))

        hold_tokens(0)

        def held_piece(i, unused):
            multiply(held_ref.at[i], i % SPLIT)

            @pl.when(i == SPLIT - 1)
            def _():
                finish(0)

            return unused

        def more_piece(i, unused):
            multiply(more_ref.at[i], (EARLY + i) % SPLIT)
            return unused

        extra = lax.shift_right_logical(hid, 16)
        lax.fori_loop(0, EARLY + extra, held_piece, 0)
        lax.fori_loop(0, MORE + extra, more_piece, 0)

        def piece(i, unused):
            bring(i).wait()
            at = first + i
            multiply(w_ref.at[i], at % SPLIT)

            @pl.when(at % SPLIT == SPLIT - 1)
            def _():
                finish((at // SPLIT) * ROWS)

            return unused

        lax.fori_loop(0, late - 1 + extra, piece, 0)
        bring(late - 1).wait()
        multiply(w_ref.at[late - 1], SPLIT - 1, last=True)
        finish(((first + late - 1) // SPLIT) * ROWS)

    pl.run_scoped(run, *[pltpu.ACC(m)((size, SIDE), F32) for m in range(UNITS) for size in (tokens, 2 * SIDE)])


def hidden_grad_call(n, parts, near, swap, weight, held, more):
    ff, width = weight.shape
    tokens = 2 * near.shape[0]
    share = tokens // parts
    late = ff // ROWS * SPLIT - EARLY - MORE
    outs = pl.pallas_call(
        functools.partial(hidden_grad_kernel, n, parts),
        out_shape=(
            jax.ShapeDtypeStruct((tokens, width), BF16),
            jax.ShapeDtypeStruct((share, ff), F32),
            *[jax.ShapeDtypeStruct((share, ff), BF16)] * (parts - 1),
        ),
        in_specs=[in_vmem()] * 2 + [anywhere()] + [in_vmem()] * 2,
        out_specs=(in_vmem(),) * (parts + 1),
        scratch_shapes=[
            VMEM((late, ROWS, width // SPLIT), BF16),
            VMEM((width, SIDE), BF16),
            pltpu.SemaphoreType.DMA((late,)),
        ],
        compiler_params=params(32),
        cost_estimate=pl.CostEstimate(
            flops=2 * tokens * width * ff, transcendentals=0, bytes_accessed=2 * width * ff
        ),
        name="hidden_grad",
    )(near, swap, in_hbm(weight), held, more)
    return outs[0], outs[1], outs[2:]


def weight_grad_kernel(sizes, hidden_ref, g_ref, out_ref, buf, sems):
    copies = []
    at = 0
    for i, size in enumerate(sizes):
        rows = pl.ds(at, size)
        buf[rows] = contract_rows(hidden_ref[:, rows], g_ref[...]).astype(BF16)
        copy = pltpu.make_async_copy(buf.at[rows], out_ref.at[rows], sems.at[i])
        copy.start()
        copies.append(copy)
        at += size
    for copy in copies:
        copy.wait()


def weight_grad_call(hidden, g):
    tokens, ff = hidden.shape
    width = g.shape[1]
    sizes = [ff // BLOCKS] * BLOCKS
    return pl.pallas_call(
        functools.partial(weight_grad_kernel, sizes),
        out_shape=jax.ShapeDtypeStruct((ff, width), BF16),
        in_specs=[in_vmem()] * 2,
        out_specs=anywhere(),
        scratch_shapes=[VMEM((ff, width), BF16), pltpu.SemaphoreType.DMA((len(sizes),))],
        compiler_params=params(48),
        cost_estimate=pl.CostEstimate(
            flops=2 * tokens * width * ff, transcendentals=0, bytes_accessed=2 * width * ff
        ),
        name="weight_grad",
    )(hidden, g)


def sum_kernel(own_ref, slope_ref, *refs):
    total = own_ref[...]
    for ref in refs[:-1]:
        total = total + ref[...].astype(F32)
    refs[-1][...] = (total * slope_ref[...]).astype(BF16)


def sum_call(own, slope, received):
    return pl.pallas_call(
        sum_kernel,
        out_shape=jax.ShapeDtypeStruct(own.shape, BF16),
        in_specs=[in_vmem()] * (2 + len(received)),
        out_specs=in_vmem(),
        compiler_params=params(8),
        name="total",
    )(own, slope, *received)


def ring(n, parts, grad_out, pre_act, weight):
    def swap(value, axis, size, k):
        return lax.ppermute(value, axis, [(i, i ^ k) for i in range(size)])

    far = []
    for k in range(2, n, 2):
        far.append(swap(grad_out, "hid", n, k))
    hidden, slope, own_rows, held = gelu_call(parts, pre_act, grad_out, weight)
    near = join_call([own_rows, *far])
    other = swap(near, "hid", n, 1)
    more = fetch_call(near, weight)
    g, own, sends = hidden_grad_call(n, parts, near, other, weight, held, more)
    received = [swap(s, "wid", parts, k + 1) for k, s in enumerate(sends)]
    grad_w = weight_grad_call(hidden, g)
    return (sum_call(own, slope, received), grad_w)


def power_of_two(size):
    return size & (size - 1) == 0


def solution(mesh):
    n, parts = mesh.shape["hid"], mesh.shape["wid"]

    def local(grad_out, pre_act, weight):
        ff, width = weight.shape
        small = power_of_two(n) and power_of_two(parts) and parts < n <= 8
        fits = ff % ROWS == 0 and ff >= 3 * ROWS and ff % (BLOCKS * 128) == 0 and width % (SPLIT * SIDE) == 0
        if small and fits and ff * width * 2 <= 40 * 2**20:
            return ring(n, parts, grad_out, pre_act, weight)
        return plain(grad_out, pre_act, weight)

    return jax.shard_map(
        local,
        mesh=mesh,
        in_specs=(P("hid", "wid"), P(None, "hid"), P("hid", "wid")),
        out_specs=(P("wid", "hid"), P("hid", "wid")),
        check_vma=False,
    )
```
